768 devices in a mesh: dom: 96 (over z, y_lo, core), st: 8 (over y_hi, x).
Axes of the slice: x: 4, y: 8 (y_hi: 2, y_lo: 4; y = y_hi * 4 + y_lo), z: 12, core: 2. Of those that a mesh axis runs over, the one named last changes fastest.
Arguments:
- orbitals: bfloat16 [384, 196608], P('st', 'dom')
- cell_matrix: bfloat16 [512, 512], replicated
- connectivity: int32 [1536, 512], P('dom'), may hold values from 0 to 2303, as said below
- surface_nodes: int32 [96, 256], P('dom'), may hold values from 0 to 2047, as said below
- cell_scale: float32 [1536], P('dom'), may hold values from 0.3 to 3
- potential: float32 [196608], P('dom'), may hold values from -1 to 2
Outputs:
- rotated_states: bfloat16 [384, 196608], P('st', 'dom')
The draws below stay inside these ranges and needn't reach their ends.
Inputs may be any that keep to these rules, and one draw needn't show every extreme that they name: `connectivity`: within a cell all 512 numbers differ. In each domain the first 12 cells name only the domain's own nodes (numbers below 2048); the others may also name the 256 shared-surface nodes of the next domain. `surface_nodes`: each row names 256 different nodes.
All inputs are finite; a program needn't handle non-finite values.
Results may differ from the reference program's by a relative error of at most 0.002.
The reference program's roundings to bfloat16 on the way count: a program that leaves them out, or rounds other values in their place, can miss the bound.
Values may be sent and summed in bfloat16 or wider, within the bound.
No kernel may reach another device: no remote copies, remote signals or barrier semaphores. Data moves between devices by JAX's collectives and lax.ppermute only.
A program may use at most 32 MiB of HBM per device.

```python
import math
import jax
import jax.numpy as jnp
from jax import lax

NODE_CELL = 512
STATES = 384
NODES_DEV = 2048
CELLS_DEV = 16
DEGREE = 3
ROOT_ITERS = 4
SURF = 256
DOMAINS = 96
NODES = 196608
CELLS = 1536
N_DOM = 96


def draw_orbitals(key, part):
    key_values, key_scales = jax.random.split(key)
    key_domain = jax.random.fold_in(key, 7)
    key_heavy = jax.random.fold_in(key, 11)
    values = jnp.clip(jax.random.normal(key_values, (STATES, NODES), jnp.float32), -6.0, 6.0)
    scales = jnp.exp(jax.random.uniform(key_scales, (STATES, 1), jnp.float32, 0.0, math.log(3.0)))
    domain_amp = jnp.exp(jax.random.uniform(key_domain, (DOMAINS,), jnp.float32, 0.0, math.log(4.0)))
    heavy = jax.random.randint(key_heavy, (), 0, DOMAINS, dtype=jnp.int32)
    domain_ids = jnp.arange(DOMAINS, dtype=jnp.int32)
    domain_amp = jnp.where(domain_ids == heavy, 4.0, domain_amp)
    node_amp = jnp.repeat(domain_amp, NODES_DEV)[None, :]
    return (values * scales * node_amp).astype(jnp.bfloat16)


def draw_cell_matrix(key, part):
    base = jax.random.normal(key, (NODE_CELL, NODE_CELL), jnp.float32)
    base = base * (0.7 / math.sqrt(NODE_CELL))
    row_ids = lax.broadcasted_iota(jnp.int32, (NODE_CELL, NODE_CELL), 0)
    col_ids = lax.broadcasted_iota(jnp.int32, (NODE_CELL, NODE_CELL), 1)
    diagonal = jnp.where(row_ids == col_ids, 2.0, 0.0)
    return (0.5 * (base + base.T) + diagonal).astype(jnp.bfloat16)


def draw_connectivity(key, part):
    width_all = NODES_DEV + SURF
    col_ids = jnp.arange(width_all, dtype=jnp.int32)[None, :]
    cell_ids = jnp.arange(CELLS, dtype=jnp.int32)[:, None]
    scores = jax.random.randint(key, (CELLS, width_all), 0, 65536, dtype=jnp.int32) * 8192 + col_ids
    inner = cell_ids % CELLS_DEV < CELLS_DEV - CELLS_DEV // 4
    is_ghost = col_ids >= NODES_DEV
    scores = jnp.where(inner & is_ghost, scores + 1073741824, scores)
    forced = (cell_ids == CELLS_DEV - 1) & ((col_ids == 0) | (col_ids == width_all - 1))
    scores = jnp.where(forced, -1, scores)
    order = jnp.argsort(scores, axis=1, stable=True)
    return order[:, :NODE_CELL].astype(jnp.int32)


def draw_surface_nodes(key, part):
    col_ids = jnp.arange(NODES_DEV, dtype=jnp.int32)[None, :]
    row_ids = jnp.arange(DOMAINS, dtype=jnp.int32)[:, None]
    scores = jax.random.randint(key, (DOMAINS, NODES_DEV), 0, 65536, dtype=jnp.int32) * 8192 + col_ids
    forced = (row_ids == 0) & ((col_ids == 0) | (col_ids == NODES_DEV - 1))
    scores = jnp.where(forced, -1, scores)
    order = jnp.argsort(scores, axis=1, stable=True)
    return order[:, :SURF].astype(jnp.int32)


def levels(rng, extent, pieces, least, high):
    loudness = 1.0
    for dim, shards_of in pieces:
        draws = jax.random.uniform(jax.random.fold_in(jax.random.fold_in(rng, 6), dim), (shards_of,), jnp.float32, least / len(pieces), high / len(pieces))
        loudness = loudness * jnp.repeat(jnp.exp(draws), extent[dim] // shards_of).reshape((-1,) + (1,) * (len(extent) - 1 - dim))
    return loudness


def setup_inputs(seed: int = 0) -> dict:
    streams_of = jax.random.split(jax.random.key(seed), 7)
    return {
        "orbitals": draw_orbitals(jax.random.fold_in(streams_of[6], 71), 0),
        "cell_matrix": draw_cell_matrix(jax.random.fold_in(streams_of[6], 71), 0),
        "connectivity": draw_connectivity(jax.random.fold_in(streams_of[6], 71), 0),
        "surface_nodes": draw_surface_nodes(jax.random.fold_in(streams_of[6], 71), 0),
        "cell_scale": jnp.clip(jnp.exp(math.log(3.0) - 2.3025851 * jax.random.uniform(streams_of[4], (CELLS,), jnp.float32) ** levels(streams_of[4], (CELLS,), ((0, 96),), -0.2, 0.2)), 0.3, 3.0),
        "potential": jnp.clip(-1.0 + 3.0 * jax.random.uniform(streams_of[5], (NODES,), jnp.float32) ** levels(streams_of[5], (NODES,), ((0, 96),), -0.2, 0.2), -1.0, 2.0),
    }


center = 7.0
half_width = 6.0
epsilon = 1e-06

def apply_hamiltonian(values, global_conn, cell_scale, potential, cell_matrix):
    padded = jnp.concatenate([values, jnp.zeros((values.shape[0], 1), values.dtype)], axis=1)
    totals = jnp.zeros(padded.shape, jnp.float32)

    def one_domain(domain, totals):
        indices = global_conn[domain]
        gathered = padded[:, indices]
        products = jnp.dot(gathered.reshape(-1, NODE_CELL), cell_matrix, preferred_element_type=jnp.float32)
        scales = lax.dynamic_slice_in_dim(cell_scale, domain * CELLS_DEV, CELLS_DEV)
        products = products.reshape(values.shape[0], CELLS_DEV, NODE_CELL) * scales[None, :, None]
        return totals.at[:, indices].add(products)
    totals = lax.fori_loop(0, N_DOM, one_domain, totals)
    return totals[:, :NODES] + potential[None, :] * values.astype(jnp.float32)

def newton_root(gram):
    highest = lax.Precision.HIGHEST
    scale_sum = jnp.sqrt(jnp.sum(gram * gram)) + epsilon
    identity = jnp.eye(STATES, dtype=jnp.float32)
    growing = gram / scale_sum
    inverse = identity
    for iteration in range(ROOT_ITERS):
        factor = 1.5 * identity - 0.5 * jnp.dot(inverse, growing, precision=highest)
        growing = jnp.dot(growing, factor, precision=highest)
        inverse = jnp.dot(factor, inverse, precision=highest)
    return (inverse, scale_sum)

def reference(orbitals, cell_matrix, connectivity, surface_nodes, cell_scale, potential):
    domains = jnp.arange(N_DOM, dtype=jnp.int32)
    upper_ids = jnp.roll(surface_nodes, -1, axis=0) + (domains[:, None] + 1) * NODES_DEV
    upper_ids = jnp.where(domains[:, None] == N_DOM - 1, NODES, upper_ids)
    own_nodes = domains[:, None] * NODES_DEV + jnp.arange(NODES_DEV, dtype=jnp.int32)[None, :]
    ext_map = jnp.concatenate([own_nodes, upper_ids], axis=1).astype(jnp.int32)
    local_conn = connectivity.reshape(N_DOM, CELLS_DEV * NODE_CELL).astype(jnp.int32)
    global_conn = jnp.take_along_axis(ext_map, local_conn, axis=1).reshape(N_DOM, CELLS_DEV, NODE_CELL)
    older = orbitals
    newest = orbitals
    for degree_step in range(DEGREE):
        image = apply_hamiltonian(newest, global_conn, cell_scale, potential, cell_matrix)
        shifted = (image - center * newest.astype(jnp.float32)) / half_width
        if degree_step == 0:
            fresh = shifted
        else:
            fresh = 2.0 * shifted - older.astype(jnp.float32)
        older = newest
        newest = fresh.astype(jnp.bfloat16)
    gram = jnp.dot(newest, newest.T, preferred_element_type=jnp.float32)
    inverse, scale_sum = newton_root(gram)
    rotation = (inverse * jnp.sqrt(NODES / scale_sum)).astype(jnp.bfloat16)
    return jnp.dot(rotation.T, newest, preferred_element_type=jnp.float32).astype(jnp.bfloat16)
```

```python
import functools
import jax
import jax.numpy as jnp
from jax import lax
from jax.experimental import pallas as pl
from jax.experimental.pallas import tpu as pltpu
from jax.sharding import Mesh
from jax.sharding import PartitionSpec as P

DEGREE = 3
ROOT_ITERS = 4
LOW = 256


center = 7.0
half_width = 6.0
epsilon = 1e-06


def tile_rows(row, rows):
    return jnp.broadcast_to(row, (rows, row.shape[1]))


def one_hot(low16):
    base = lax.broadcasted_iota(jnp.int32, low16.shape, 0)
    pieces = []
    for start in range(0, LOW, low16.shape[0]):
        ids = (base + start).astype(jnp.float32).astype(jnp.bfloat16)
        pieces.append(jnp.where(low16 == ids, jnp.bfloat16(1), jnp.bfloat16(0)))
    return jnp.concatenate(pieces, axis=0)


def pick_block(high, blocks):
    level, bit = list(blocks), 0
    while len(level) > 1:
        mask = (high >> bit) & 1 == 1
        nxt = []
        for i in range(0, len(level) - 1, 2):
            nxt.append(jnp.where(mask, level[i + 1], level[i]))
        if len(level) % 2:
            nxt.append(level[-1])
        level, bit = nxt, bit + 1
    return level[0]


def cells_body(n_add, first, count, n_blocks, scale_ref, *refs):
    conn_ref, matrix_ref = refs[0], refs[1]
    srcs = refs[2 : 2 + (2 if n_blocks > 8 else 1)]
    pos = 2 + len(srcs)
    adds = refs[pos : pos + n_add]
    out_ref, oh_ref, got_ref = refs[pos + n_add :][:3]
    states = srcs[0].shape[0]
    width = conn_ref.shape[1]
    columns = [srcs[0][:, b * LOW : (b + 1) * LOW] for b in range(srcs[0].shape[1] // LOW)]
    if n_blocks > 8:
        columns.append(srcs[1][...])
    stacked = jnp.concatenate(columns, axis=0)
    for i in range(count):
        row = conn_ref[first + i : first + i + 1, :]
        low16 = tile_rows(row & (LOW - 1), 16).astype(jnp.float32).astype(jnp.bfloat16)
        hot = one_hot(low16)
        oh_ref[i] = hot
        high = tile_rows(row >> 8, states)
        wide = jnp.dot(stacked, hot, preferred_element_type=jnp.float32)
        blocks = [wide[b * states : (b + 1) * states] for b in range(n_blocks)]
        got_ref[i * states : (i + 1) * states, :] = pick_block(high, blocks).astype(jnp.bfloat16)
    lefts = []
    for i in range(count):
        product = jnp.dot(
            got_ref[i * states : (i + 1) * states, :], matrix_ref[...], preferred_element_type=jnp.float32
        )
        product = product * scale_ref[first + i]
        upper = product.astype(jnp.bfloat16)
        lower = (product - upper.astype(jnp.float32)).astype(jnp.bfloat16)
        row = conn_ref[first + i : first + i + 1, :]
        high16 = tile_rows(row >> 8, states).astype(jnp.float32).astype(jnp.bfloat16)
        zero = jnp.zeros_like(upper)
        masks = [high16 == jnp.bfloat16(b) for b in range(n_blocks)]
        lefts.append(jnp.concatenate([jnp.where(m, part, zero) for part in (upper, lower) for m in masks], axis=0))
    left = jnp.concatenate(lefts, axis=1)
    right = jnp.concatenate([oh_ref[i] for i in range(count)], axis=1)
    total = lax.dot_general(left, right, (((1,), (1,)), ((), ())), preferred_element_type=jnp.float32)
    total = total[: n_blocks * states] + total[n_blocks * states :]
    for b in range(n_blocks):
        value = total[b * states : (b + 1) * states]
        for a in adds:
            if b * LOW < a.shape[1]:
                value = value + a[:, b * LOW : (b + 1) * LOW]
        out_ref[:, b * LOW : (b + 1) * LOW] = value


def cells(first, count, scale, conn, matrix, srcs, adds=()):
    states = srcs[0].shape[0]
    n_blocks = sum(s.shape[1] for s in srcs) // LOW
    smem = pl.BlockSpec(memory_space=pltpu.SMEM)
    vmem = pl.BlockSpec(memory_space=pltpu.VMEM)
    width = conn.shape[1]
    rows = states * n_blocks
    flops = 2 * count * width * (rows * LOW * 3 + states * width)
    return pl.pallas_call(
        functools.partial(cells_body, len(adds), first, count, n_blocks),
        out_shape=jax.ShapeDtypeStruct((states, n_blocks * LOW), jnp.float32),
        in_specs=[smem] + [vmem] * (2 + len(srcs) + len(adds)),
        out_specs=vmem,
        scratch_shapes=[
            pltpu.VMEM((count, LOW, width), jnp.bfloat16),
            pltpu.VMEM((count * states, width), jnp.bfloat16),
        ],
        cost_estimate=pl.CostEstimate(flops=3 * flops, bytes_accessed=3 << 20, transcendentals=0),
        name=f"cells_{first}_{count}",
    )(scale, conn, matrix, *srcs, *adds)


def combine_body(first_step, last_step, total_ref, back_ref, surf_ref, pot_ref, new_ref, *refs):
    refs = list(refs)
    old_ref = None if first_step else refs.pop(0)
    out_ref = refs.pop(0)
    states, nodes = new_ref.shape
    n_blocks = nodes // LOW
    row = surf_ref[...]
    low16 = tile_rows(row & (LOW - 1), 16).astype(jnp.float32).astype(jnp.bfloat16)
    high16 = tile_rows(row >> 8, states).astype(jnp.float32).astype(jnp.bfloat16)
    hot = one_hot(low16)
    back = back_ref[...]
    upper = back.astype(jnp.bfloat16)
    lower = (back - upper.astype(jnp.float32)).astype(jnp.bfloat16)
    zero = jnp.zeros_like(upper)
    masks = [high16 == jnp.bfloat16(b) for b in range(n_blocks)]
    left = jnp.concatenate([jnp.where(m, part, zero) for part in (upper, lower) for m in masks], axis=0)
    added = lax.dot_general(left, hot, (((1,), (1,)), ((), ())), preferred_element_type=jnp.float32)
    added = added[: n_blocks * states] + added[n_blocks * states :]
    fresh_blocks = []
    for b in range(n_blocks):
        span = slice(b * LOW, (b + 1) * LOW)
        values = new_ref[:, span].astype(jnp.float32)
        image = total_ref[:, span] + added[b * states : (b + 1) * states]
        image = image + pot_ref[:, span] * values
        fresh = (image - center * values) / half_width
        if not first_step:
            fresh = 2.0 * fresh - old_ref[:, span].astype(jnp.float32)
        fresh = fresh.astype(jnp.bfloat16)
        out_ref[:, span] = fresh
        fresh_blocks.append(fresh)
    if not last_step:
        refs.pop(0)[...] = edge_values(row, hot, fresh_blocks)


def edge_values(row, hot, columns):
    states = columns[0].shape[0]
    wide = jnp.dot(jnp.concatenate(columns, axis=0), hot, preferred_element_type=jnp.float32)
    blocks = [wide[b * states : (b + 1) * states] for b in range(len(columns))]
    return pick_block(tile_rows(row >> 8, states), blocks).astype(jnp.bfloat16)


def combine(total, back, surf, pot, newest, older, last_step):
    first_step = older is None
    states, nodes = newest.shape
    edge = surf.shape[1]
    vmem = pl.BlockSpec(memory_space=pltpu.VMEM)
    olds = () if first_step else (older,)
    outs = [jax.ShapeDtypeStruct((states, nodes), jnp.bfloat16)]
    if not last_step:
        outs.append(jax.ShapeDtypeStruct((states, edge), jnp.bfloat16))
    return pl.pallas_call(
        functools.partial(combine_body, first_step, last_step),
        out_shape=outs,
        in_specs=[vmem] * (5 + len(olds)),
        out_specs=[vmem] * len(outs),
        cost_estimate=pl.CostEstimate(flops=1 << 28, bytes_accessed=1 << 20, transcendentals=0),
        name="combine",
    )(total, back, surf, pot, newest, *olds)


def edge_body(surf_ref, new_ref, out_ref):
    row = surf_ref[...]
    low16 = tile_rows(row & (LOW - 1), 16).astype(jnp.float32).astype(jnp.bfloat16)
    columns = [new_ref[:, b * LOW : (b + 1) * LOW] for b in range(new_ref.shape[1] // LOW)]
    out_ref[...] = edge_values(row, one_hot(low16), columns)


def edge(surf, newest):
    vmem = pl.BlockSpec(memory_space=pltpu.VMEM)
    return pl.pallas_call(
        edge_body,
        out_shape=jax.ShapeDtypeStruct((newest.shape[0], surf.shape[1]), jnp.bfloat16),
        in_specs=[vmem, vmem],
        out_specs=vmem,
        name="edge",
    )(surf, newest)


def split(a):
    upper = a.astype(jnp.bfloat16)
    return upper, (a - upper.astype(jnp.float32)).astype(jnp.bfloat16)


def product(a, b):
    (ah, al), (bh, bl) = a, b
    dot = functools.partial(jnp.dot, preferred_element_type=jnp.float32)
    return dot(ah, bh) + (dot(ah, bl) + dot(al, bh))


def rotate_body(node_total, start_ref, gram_ref, field_ref, out_ref, high_ref):
    gram = gram_ref[...]
    states = gram.shape[0]
    rows = out_ref.shape[0]
    scale_sum = jnp.sqrt(jnp.sum(gram * gram, keepdims=True)) + epsilon
    eye = (
        lax.broadcasted_iota(jnp.int32, gram.shape, 0) == lax.broadcasted_iota(jnp.int32, gram.shape, 1)
    ).astype(jnp.float32)
    growing = gram / scale_sum
    factor = 1.5 * eye - 0.5 * growing
    inverse = factor
    for iteration in range(1, ROOT_ITERS):
        parts = split(factor)
        growing = product(parts, split(growing))
        if iteration > 1:
            inverse = product(split(inverse), parts)
        factor = 1.5 * eye - 0.5 * product(split(growing), split(inverse))
    high_ref[...] = inverse
    start = pl.multiple_of(start_ref[0] * rows, 16)
    mine = high_ref[pl.ds(start, rows), :]
    mine = product(split(mine), split(factor))
    turn = (mine * jnp.sqrt(node_total / scale_sum)).astype(jnp.bfloat16)
    out_ref[...] = jnp.dot(turn, field_ref[...], preferred_element_type=jnp.float32).astype(jnp.bfloat16)


def rotate(start, gram, field, rows, node_total):
    smem = pl.BlockSpec(memory_space=pltpu.SMEM)
    vmem = pl.BlockSpec(memory_space=pltpu.VMEM)
    return pl.pallas_call(
        functools.partial(rotate_body, node_total),
        out_shape=jax.ShapeDtypeStruct((rows, field.shape[1]), jnp.bfloat16),
        in_specs=[smem, vmem, vmem],
        out_specs=vmem,
        scratch_shapes=[pltpu.VMEM(gram.shape, jnp.float32)],
        name="rotate",
    )(start, gram, field)


def behind(block, distance):
    devices = range(lax.axis_size(DOM))
    route = [(i - distance, i) for i in devices if i - distance in devices]
    return lax.ppermute(block, DOM, route)


def swap(block, axes):
    return lax.all_to_all(block, axes, 0, 0, tiled=True)


def spread(block, axes):
    return swap(jnp.broadcast_to(block[None], (lax.axis_size(axes), *block.shape)), axes)


def gram_total(rows):
    states, columns = rows.shape
    depth, pairs = lax.axis_size("z"), lax.axis_size("yh")
    part = jnp.sum(swap(rows.reshape(depth, states // depth, columns), "z"), axis=0)
    parts = spread(part, ("yl", "core", "yh"))
    parts = parts.reshape(-1, pairs, *part.shape).sum(axis=0)
    whole = spread(parts, ("z", "x")).reshape(depth, -1, *parts.shape)
    return whole.transpose(1, 2, 0, 3, 4).reshape(-1, columns)


def field_all(newest):
    other = lax.ppermute(newest, "yh", [(0, 1), (1, 0)])
    first = lax.axis_index("yh") == 0
    pair = jnp.stack([jnp.where(first, newest, other), jnp.where(first, other, newest)])
    return spread(pair, "x").reshape(-1, newest.shape[1])


def body(orbitals, cell_matrix, connectivity, surface_nodes, cell_scale, potential):
    pot = potential[None, :]
    cell_args = (cell_scale, connectivity, cell_matrix)
    cell_count = connectivity.shape[0]
    inner = cell_count - cell_count // 4
    half = inner // 2
    older, newest = None, orbitals
    boundary = edge(surface_nodes, newest)
    for degree_step in range(DEGREE):
        last = degree_step == DEGREE - 1
        ghosts = behind(boundary, -1)
        first_total = cells(0, half, *cell_args, (newest,))
        shared = cells(inner, cell_count - inner, *cell_args, (newest, ghosts))
        returned = behind(shared[:, newest.shape[1]:], 1)
        total = cells(half, inner - half, *cell_args, (newest,), (first_total, shared))
        result = combine(total, returned, surface_nodes, pot, newest, older, last)
        older, newest = newest, result[0]
        boundary = None if last else result[1]
    field = field_all(newest)
    rows = lax.dot_general(newest, field, (((1,), (1,)), ((), ())), preferred_element_type=jnp.float32)
    node_total = lax.axis_size(DOM) * orbitals.shape[1]
    start = lax.axis_index(("x", "yh")).astype(jnp.int32)[None]
    return rotate(start, gram_total(rows), field, orbitals.shape[0], node_total)


DOM = ("z", "yl", "core")
ST = ("yh", "x")


def solution(mesh):
    dom, st = mesh.shape["dom"], mesh.shape["st"]
    fine = Mesh(mesh.devices.reshape(dom // 8, 4, 2, 2, st // 2), (*DOM, *ST))
    return jax.shard_map(
        body,
        mesh=fine,
        in_specs=(P(ST, DOM), P(), P(DOM, None), P(DOM, None), P(DOM), P(DOM)),
        out_specs=P(ST, DOM),
        check_vma=False,
    )
```

```python
import functools
import jax
import jax.numpy as jnp
from jax import lax
from jax.experimental import pallas as pl
from jax.experimental.pallas import tpu as pltpu
from jax.sharding import Mesh
from jax.sharding import PartitionSpec as P

DEGREE = 3
ROOT_ITERS = 4
LOW = 256
VMEM_LIMIT = 24 << 20


center = 7.0
half_width = 6.0
epsilon = 1e-06


def tile_rows(row, rows):
    return jnp.broadcast_to(row, (rows, row.shape[1]))


def one_hot(low16):
    base = lax.broadcasted_iota(jnp.int32, low16.shape, 0)
    pieces = []
    for start in range(0, LOW, low16.shape[0]):
        ids = (base + start).astype(jnp.float32).astype(jnp.bfloat16)
        pieces.append(jnp.where(low16 == ids, jnp.bfloat16(1), jnp.bfloat16(0)))
    return jnp.concatenate(pieces, axis=0)


def pick_block(high, blocks):
    level, bit = list(blocks), 0
    while len(level) > 1:
        mask = (high >> bit) & 1 == 1
        nxt = []
        for i in range(0, len(level) - 1, 2):
            nxt.append(jnp.where(mask, level[i + 1], level[i]))
        if len(level) % 2:
            nxt.append(level[-1])
        level, bit = nxt, bit + 1
    return level[0]


def cells_body(n_add, first, count, n_blocks, scale_ref, *refs):
    conn_ref, matrix_ref = refs[0], refs[1]
    srcs = refs[2 : 2 + (2 if n_blocks > 8 else 1)]
    pos = 2 + len(srcs)
    adds = refs[pos : pos + n_add]
    out_refs = refs[pos + n_add : -2]
    oh_ref, got_ref = refs[-2:]
    states = srcs[0].shape[0]
    width = conn_ref.shape[1]
    columns = [srcs[0][:, b * LOW : (b + 1) * LOW] for b in range(srcs[0].shape[1] // LOW)]
    if n_blocks > 8:
        columns.append(srcs[1][...])
    stacked = jnp.concatenate(columns, axis=0)
    for i in range(count):
        row = conn_ref[first + i : first + i + 1, :]
        low16 = tile_rows(row & (LOW - 1), 16).astype(jnp.float32).astype(jnp.bfloat16)
        hot = one_hot(low16)
        oh_ref[i] = hot
        high = tile_rows(row >> 8, states)
        wide = jnp.dot(stacked, hot, preferred_element_type=jnp.float32)
        blocks = [wide[b * states : (b + 1) * states] for b in range(n_blocks)]
        got_ref[i * states : (i + 1) * states, :] = pick_block(high, blocks).astype(jnp.bfloat16)
    products = jnp.dot(got_ref[...], matrix_ref[...], preferred_element_type=jnp.float32)
    lefts = []
    for i in range(count):
        product = products[i * states : (i + 1) * states] * scale_ref[first + i]
        upper = product.astype(jnp.bfloat16)
        lower = (product - upper.astype(jnp.float32)).astype(jnp.bfloat16)
        row = conn_ref[first + i : first + i + 1, :]
        high16 = tile_rows(row >> 8, states).astype(jnp.float32).astype(jnp.bfloat16)
        zero = jnp.zeros_like(upper)
        masks = [high16 == jnp.bfloat16(b) for b in range(n_blocks)]
        lefts.append(jnp.concatenate([jnp.where(m, part, zero) for part in (upper, lower) for m in masks], axis=0))
    left = jnp.concatenate(lefts, axis=1)
    right = jnp.concatenate([oh_ref[i] for i in range(count)], axis=1)
    total = lax.dot_general(left, right, (((1,), (1,)), ((), ())), preferred_element_type=jnp.float32)
    total = total[: n_blocks * states] + total[n_blocks * states :]
    for b in range(n_blocks):
        value = total[b * states : (b + 1) * states]
        for a in adds:
            if b * LOW < a.shape[1]:
                value = value + a[:, b * LOW : (b + 1) * LOW]
        out_ref, place = (out_refs[0], b) if b < 8 else (out_refs[1], 0)
        out_ref[:, place * LOW : (place + 1) * LOW] = value


def cells(first, count, scale, conn, matrix, srcs, adds=()):
    states = srcs[0].shape[0]
    n_blocks = sum(s.shape[1] for s in srcs) // LOW
    smem = pl.BlockSpec(memory_space=pltpu.SMEM)
    vmem = pl.BlockSpec(memory_space=pltpu.VMEM)
    width = conn.shape[1]
    rows = states * n_blocks
    flops = 2 * count * width * (rows * LOW * 3 + states * width)
    return pl.pallas_call(
        functools.partial(cells_body, len(adds), first, count, n_blocks),
        out_shape=[jax.ShapeDtypeStruct(s.shape, jnp.float32) for s in srcs],
        in_specs=[smem] + [vmem] * (2 + len(srcs) + len(adds)),
        out_specs=[vmem] * len(srcs),
        scratch_shapes=[
            pltpu.VMEM((count, LOW, width), jnp.bfloat16),
            pltpu.VMEM((count * states, width), jnp.bfloat16),
        ],
        cost_estimate=pl.CostEstimate(flops=3 * flops, bytes_accessed=3 << 20, transcendentals=0),
        compiler_params=pltpu.CompilerParams(vmem_limit_bytes=VMEM_LIMIT),
        name=f"cells_{first}_{count}",
    )(scale, conn, matrix, *srcs, *adds)


def combine_body(first_step, last_step, side_ref, total_ref, back_ref, surf_ref, pot_ref, new_ref, *refs):
    refs = list(refs)
    old_ref = None if first_step else refs.pop(0)
    out_ref = refs.pop(0)
    states, nodes = new_ref.shape
    n_blocks = nodes // LOW
    row = surf_ref[...]
    low16 = tile_rows(row & (LOW - 1), 16).astype(jnp.float32).astype(jnp.bfloat16)
    high16 = tile_rows(row >> 8, states).astype(jnp.float32).astype(jnp.bfloat16)
    hot = one_hot(low16)
    back = back_ref[...]
    upper = back.astype(jnp.bfloat16)
    lower = (back - upper.astype(jnp.float32)).astype(jnp.bfloat16)
    zero = jnp.zeros_like(upper)
    masks = [high16 == jnp.bfloat16(b) for b in range(n_blocks)]
    left = jnp.concatenate([jnp.where(m, part, zero) for part in (upper, lower) for m in masks], axis=0)
    added = lax.dot_general(left, hot, (((1,), (1,)), ((), ())), preferred_element_type=jnp.float32)
    added = added[: n_blocks * states] + added[n_blocks * states :]
    fresh_blocks = []
    for b in range(n_blocks):
        span = slice(b * LOW, (b + 1) * LOW)
        values = new_ref[:, span].astype(jnp.float32)
        image = total_ref[:, span] + added[b * states : (b + 1) * states]
        image = image + pot_ref[:, span] * values
        fresh = (image - center * values) / half_width
        if not first_step:
            fresh = 2.0 * fresh - old_ref[:, span].astype(jnp.float32)
        fresh = fresh.astype(jnp.bfloat16)
        if not last_step:
            out_ref[:, span] = fresh
        fresh_blocks.append(fresh)
    if last_step:
        first = side_ref[0] == 0
        middle = n_blocks // 2
        for b in range(middle):
            span = slice(b * LOW, (b + 1) * LOW)
            early, late = fresh_blocks[b], fresh_blocks[middle + b]
            out_ref[:, span] = jnp.where(first, early, late)
            refs[0][:, span] = jnp.where(first, late, early)
    else:
        refs[0][...] = edge_values(row, hot, fresh_blocks)


def edge_values(row, hot, columns):
    states = columns[0].shape[0]
    wide = jnp.dot(jnp.concatenate(columns, axis=0), hot, preferred_element_type=jnp.float32)
    blocks = [wide[b * states : (b + 1) * states] for b in range(len(columns))]
    return pick_block(tile_rows(row >> 8, states), blocks).astype(jnp.bfloat16)


def combine(side, total, back, surf, pot, newest, older, last_step):
    first_step = older is None
    states, nodes = newest.shape
    edge = surf.shape[1]
    vmem = pl.BlockSpec(memory_space=pltpu.VMEM)
    olds = () if first_step else (older,)
    if last_step:
        outs = [jax.ShapeDtypeStruct((states, nodes // 2), jnp.bfloat16)] * 2
    else:
        outs = [jax.ShapeDtypeStruct((states, n), jnp.bfloat16) for n in (nodes, edge)]
    smem = pl.BlockSpec(memory_space=pltpu.SMEM)
    return pl.pallas_call(
        functools.partial(combine_body, first_step, last_step),
        out_shape=outs,
        in_specs=[smem] + [vmem] * (5 + len(olds)),
        out_specs=[vmem] * len(outs),
        cost_estimate=pl.CostEstimate(flops=1 << 28, bytes_accessed=1 << 20, transcendentals=0),
        compiler_params=pltpu.CompilerParams(vmem_limit_bytes=VMEM_LIMIT),
        name="combine",
    )(side, total, back, surf, pot, newest, *olds)


def edge_body(surf_ref, new_ref, out_ref):
    row = surf_ref[...]
    low16 = tile_rows(row & (LOW - 1), 16).astype(jnp.float32).astype(jnp.bfloat16)
    columns = [new_ref[:, b * LOW : (b + 1) * LOW] for b in range(new_ref.shape[1] // LOW)]
    out_ref[...] = edge_values(row, one_hot(low16), columns)


def edge(surf, newest):
    vmem = pl.BlockSpec(memory_space=pltpu.VMEM)
    return pl.pallas_call(
        edge_body,
        out_shape=jax.ShapeDtypeStruct((newest.shape[0], surf.shape[1]), jnp.bfloat16),
        in_specs=[vmem, vmem],
        out_specs=vmem,
        compiler_params=pltpu.CompilerParams(vmem_limit_bytes=VMEM_LIMIT),
        name="edge",
    )(surf, newest)


def split(a):
    upper = a.astype(jnp.bfloat16)
    return upper, (a - upper.astype(jnp.float32)).astype(jnp.bfloat16)


def product(a, b):
    rows = a.shape[0]
    (ah, al), (bh, bl) = split(a), split(b)
    dot = functools.partial(jnp.dot, preferred_element_type=jnp.float32)
    return dot(jnp.concatenate([ah, al, ah], axis=1), jnp.concatenate([bh, bh, bl], axis=0))


def arrange_body(side_ref, keep_ref, other_ref, out_ref):
    first = side_ref[0] == 0
    states = keep_ref.shape[0]
    keep, other = keep_ref[...], other_ref[...]
    early, late = jnp.where(first, keep, other), jnp.where(first, other, keep)
    for i in range(out_ref.shape[0]):
        out_ref[i, :states] = early
        out_ref[i, states:] = late


def arrange(side, keep, other, copies):
    smem = pl.BlockSpec(memory_space=pltpu.SMEM)
    vmem = pl.BlockSpec(memory_space=pltpu.VMEM)
    states, nodes = keep.shape
    return pl.pallas_call(
        arrange_body,
        out_shape=jax.ShapeDtypeStruct((copies, 2 * states, nodes), jnp.bfloat16),
        in_specs=[smem, vmem, vmem],
        out_specs=vmem,
        compiler_params=pltpu.CompilerParams(vmem_limit_bytes=VMEM_LIMIT),
        name="arrange",
    )(side, keep, other)


def rotate_body(node_total, side_ref, gram_ref, field_ref, keep_ref, send_ref, high_ref, turned_ref):
    gram = gram_ref[...]
    rows = turned_ref.shape[0]
    half = rows // 2
    scale_sum = jnp.sqrt(jnp.sum(gram * gram, keepdims=True)) + epsilon
    eye = (
        lax.broadcasted_iota(jnp.int32, gram.shape, 0) == lax.broadcasted_iota(jnp.int32, gram.shape, 1)
    ).astype(jnp.float32)
    growing = gram / scale_sum
    factor = 1.5 * eye - 0.5 * growing
    inverse = factor
    for iteration in range(1, ROOT_ITERS):
        growing = product(factor, growing)
        if iteration > 1:
            inverse = product(inverse, factor)
        factor = 1.5 * eye - 0.5 * product(growing, inverse)
    high_ref[...] = inverse
    mine = high_ref[pl.ds(pl.multiple_of(side_ref[1] * rows, 32), rows), :]
    mine = product(mine, factor)
    turn = (mine * jnp.sqrt(node_total / scale_sum)).astype(jnp.bfloat16)
    turned_ref[...] = jnp.dot(turn, field_ref[...], preferred_element_type=jnp.float32).astype(jnp.bfloat16)
    side = side_ref[0]
    keep_ref[...] = turned_ref[pl.ds(pl.multiple_of(side * half, 16), half), :]
    send_ref[...] = turned_ref[pl.ds(pl.multiple_of((1 - side) * half, 16), half), :]


def rotate(side, gram, field, rows, node_total):
    smem = pl.BlockSpec(memory_space=pltpu.SMEM)
    vmem = pl.BlockSpec(memory_space=pltpu.VMEM)
    nodes = field.shape[1]
    return pl.pallas_call(
        functools.partial(rotate_body, node_total),
        out_shape=[jax.ShapeDtypeStruct((rows // 2, nodes), jnp.bfloat16)] * 2,
        in_specs=[smem, vmem, vmem],
        out_specs=[vmem] * 2,
        scratch_shapes=[pltpu.VMEM(gram.shape, jnp.float32), pltpu.VMEM((rows, nodes), jnp.bfloat16)],
        compiler_params=pltpu.CompilerParams(vmem_limit_bytes=VMEM_LIMIT),
        name="rotate",
    )(side, gram, field)


def behind(block, distance):
    devices = range(lax.axis_size(DOM))
    route = [(i - distance, i) for i in devices if i - distance in devices]
    return lax.ppermute(block, DOM, route)


def swap(block, axes):
    return lax.all_to_all(block, axes, 0, 0, tiled=True)


def spread(block, axes):
    return swap(jnp.broadcast_to(block[None], (lax.axis_size(axes), *block.shape)), axes)


def gram_total(rows):
    states, columns = rows.shape
    near = ("yl", "core", "yh")
    count = lax.axis_size(near)
    part = jnp.sum(swap(rows.reshape(count, states // count, columns), near), axis=0)
    part = jnp.sum(spread(part, "z"), axis=0)
    block = spread(part, near).reshape(states, columns)
    return spread(block, "x").reshape(-1, columns)


def turn_over(block):
    return lax.ppermute(block, "yh", [(0, 1), (1, 0)])


def body(orbitals, cell_matrix, connectivity, surface_nodes, cell_scale, potential):
    pot = potential[None, :]
    cell_args = (cell_scale, connectivity, cell_matrix)
    cell_count = connectivity.shape[0]
    inner = cell_count - cell_count // 4
    half = inner // 2
    side = jnp.stack([lax.axis_index("yh"), lax.axis_index("x")]).astype(jnp.int32)
    older, newest = None, orbitals
    boundary = edge(surface_nodes, newest)
    for degree_step in range(DEGREE):
        last = degree_step == DEGREE - 1
        ghosts = behind(boundary, -1)
        first_total = cells(0, half, *cell_args, (newest,))
        shared = cells(inner, cell_count - inner, *cell_args, (newest, ghosts))
        returned = behind(shared[1], 1)
        total = cells(half, inner - half, *cell_args, (newest,), (first_total[0], shared[0]))[0]
        result = combine(side, total, returned, surface_nodes, pot, newest, older, last)
        older, (newest, boundary) = newest, result
    keep, send = newest, boundary
    copies = lax.axis_size("x")
    pair = arrange(side, keep, turn_over(send), copies)
    field = swap(pair, "x").reshape(-1, keep.shape[1])
    rows = lax.dot_general(pair[0], field, (((1,), (1,)), ((), ())), preferred_element_type=jnp.float32)
    node_total = lax.axis_size(DOM) * orbitals.shape[1]
    keep, send = rotate(side, gram_total(rows), field, rows.shape[0], node_total)
    other = turn_over(send)
    first = side[0] == 0
    return jnp.where(first, jnp.concatenate([keep, other], axis=1), jnp.concatenate([other, keep], axis=1))


DOM = ("z", "yl", "core")
ST = ("yh", "x")


def solution(mesh):
    dom, st = mesh.shape["dom"], mesh.shape["st"]
    fine = Mesh(mesh.devices.reshape(dom // 8, 4, 2, 2, st // 2), (*DOM, *ST))
    return jax.shard_map(
        body,
        mesh=fine,
        in_specs=(P(ST, DOM), P(), P(DOM, None), P(DOM, None), P(DOM), P(DOM)),
        out_specs=P(ST, DOM),
        check_vma=False,
    )
```

```python
import functools
import jax
import jax.numpy as jnp
from jax import lax
from jax.experimental import pallas as pl
from jax.experimental.pallas import tpu as pltpu
from jax.sharding import Mesh
from jax.sharding import PartitionSpec as P

DEGREE = 3
ROOT_ITERS = 4
LOW = 256
VMEM_LIMIT = 24 << 20


center = 7.0
half_width = 6.0
epsilon = 1e-06


def tile_rows(row, rows):
    return jnp.broadcast_to(row, (rows, row.shape[1]))


def one_hot(low16):
    base = lax.broadcasted_iota(jnp.int32, low16.shape, 0)
    pieces = []
    for start in range(0, LOW, low16.shape[0]):
        ids = (base + start).astype(jnp.float32).astype(jnp.bfloat16)
        pieces.append(jnp.where(low16 == ids, jnp.bfloat16(1), jnp.bfloat16(0)))
    return jnp.concatenate(pieces, axis=0)


def pick_block(high, blocks):
    level, bit = list(blocks), 0
    while len(level) > 1:
        mask = (high >> bit) & 1 == 1
        nxt = []
        for i in range(0, len(level) - 1, 2):
            nxt.append(jnp.where(mask, level[i + 1], level[i]))
        if len(level) % 2:
            nxt.append(level[-1])
        level, bit = nxt, bit + 1
    return level[0]


def cells_body(n_add, first, count, n_blocks, scale_ref, *refs):
    conn_ref, matrix_ref = refs[0], refs[1]
    srcs = refs[2 : 2 + (2 if n_blocks > 8 else 1)]
    pos = 2 + len(srcs)
    adds = refs[pos : pos + n_add]
    out_refs = refs[pos + n_add : -2]
    oh_ref, got_ref = refs[-2:]
    states = srcs[0].shape[0]
    width = conn_ref.shape[1]
    columns = [srcs[0][:, b * LOW : (b + 1) * LOW] for b in range(srcs[0].shape[1] // LOW)]
    if n_blocks > 8:
        columns.append(srcs[1][...])
    stacked = jnp.concatenate(columns, axis=0)
    for i in range(count):
        row = conn_ref[first + i : first + i + 1, :]
        low16 = tile_rows(row & (LOW - 1), 16).astype(jnp.float32).astype(jnp.bfloat16)
        hot = one_hot(low16)
        oh_ref[i] = hot
        high = tile_rows(row >> 8, states)
        wide = jnp.dot(stacked, hot, preferred_element_type=jnp.float32)
        blocks = [wide[b * states : (b + 1) * states] for b in range(n_blocks)]
        got_ref[i * states : (i + 1) * states, :] = pick_block(high, blocks).astype(jnp.bfloat16)
    products = jnp.dot(got_ref[...], matrix_ref[...], preferred_element_type=jnp.float32)
    lefts = []
    for i in range(count):
        product = products[i * states : (i + 1) * states] * scale_ref[first + i]
        upper = product.astype(jnp.bfloat16)
        lower = (product - upper.astype(jnp.float32)).astype(jnp.bfloat16)
        row = conn_ref[first + i : first + i + 1, :]
        high16 = tile_rows(row >> 8, states).astype(jnp.float32).astype(jnp.bfloat16)
        zero = jnp.zeros_like(upper)
        masks = [high16 == jnp.bfloat16(b) for b in range(n_blocks)]
        lefts.append(jnp.concatenate([jnp.where(m, part, zero) for part in (upper, lower) for m in masks], axis=0))
    left = jnp.concatenate(lefts, axis=1)
    right = jnp.concatenate([oh_ref[i] for i in range(count)], axis=1)
    total = lax.dot_general(left, right, (((1,), (1,)), ((), ())), preferred_element_type=jnp.float32)
    total = total[: n_blocks * states] + total[n_blocks * states :]
    for b in range(n_blocks):
        value = total[b * states : (b + 1) * states]
        for a in adds:
            if b * LOW < a.shape[1]:
                value = value + a[:, b * LOW : (b + 1) * LOW]
        out_ref, place = (out_refs[0], b) if b < 8 else (out_refs[1], 0)
        out_ref[:, place * LOW : (place + 1) * LOW] = value


def cells(first, count, scale, conn, matrix, srcs, adds=()):
    states = srcs[0].shape[0]
    n_blocks = sum(s.shape[1] for s in srcs) // LOW
    smem = pl.BlockSpec(memory_space=pltpu.SMEM)
    vmem = pl.BlockSpec(memory_space=pltpu.VMEM)
    width = conn.shape[1]
    rows = states * n_blocks
    flops = 2 * count * width * (rows * LOW * 3 + states * width)
    return pl.pallas_call(
        functools.partial(cells_body, len(adds), first, count, n_blocks),
        out_shape=[jax.ShapeDtypeStruct(s.shape, jnp.float32) for s in srcs],
        in_specs=[smem] + [vmem] * (2 + len(srcs) + len(adds)),
        out_specs=[vmem] * len(srcs),
        scratch_shapes=[
            pltpu.VMEM((count, LOW, width), jnp.bfloat16),
            pltpu.VMEM((count * states, width), jnp.bfloat16),
        ],
        cost_estimate=pl.CostEstimate(flops=3 * flops, bytes_accessed=3 << 20, transcendentals=0),
        compiler_params=pltpu.CompilerParams(vmem_limit_bytes=VMEM_LIMIT),
        name=f"cells_{first}_{count}",
    )(scale, conn, matrix, *srcs, *adds)


def combine_body(first_step, last_step, total_ref, back_ref, surf_ref, pot_ref, new_ref, *refs):
    refs = list(refs)
    old_ref = None if first_step else refs.pop(0)
    out_ref = refs.pop(0)
    states, nodes = new_ref.shape
    n_blocks = nodes // LOW
    row = surf_ref[...]
    low16 = tile_rows(row & (LOW - 1), 16).astype(jnp.float32).astype(jnp.bfloat16)
    high16 = tile_rows(row >> 8, states).astype(jnp.float32).astype(jnp.bfloat16)
    hot = one_hot(low16)
    back = back_ref[...]
    upper = back.astype(jnp.bfloat16)
    lower = (back - upper.astype(jnp.float32)).astype(jnp.bfloat16)
    zero = jnp.zeros_like(upper)
    masks = [high16 == jnp.bfloat16(b) for b in range(n_blocks)]
    left = jnp.concatenate([jnp.where(m, part, zero) for part in (upper, lower) for m in masks], axis=0)
    added = lax.dot_general(left, hot, (((1,), (1,)), ((), ())), preferred_element_type=jnp.float32)
    added = added[: n_blocks * states] + added[n_blocks * states :]
    fresh_blocks = []
    for b in range(n_blocks):
        span = slice(b * LOW, (b + 1) * LOW)
        values = new_ref[:, span].astype(jnp.float32)
        image = total_ref[:, span] + added[b * states : (b + 1) * states]
        image = image + pot_ref[:, span] * values
        fresh = (image - center * values) / half_width
        if not first_step:
            fresh = 2.0 * fresh - old_ref[:, span].astype(jnp.float32)
        fresh = fresh.astype(jnp.bfloat16)
        if not last_step:
            out_ref[:, span] = fresh
        fresh_blocks.append(fresh)
    if last_step:
        middle = n_blocks // 2
        for part in range(2):
            block = jnp.concatenate(fresh_blocks[part * middle : (part + 1) * middle], axis=1)
            for copy in range(out_ref.shape[1]):
                out_ref[part, copy] = block
    else:
        refs[0][...] = edge_values(row, hot, fresh_blocks)


def edge_values(row, hot, columns):
    states = columns[0].shape[0]
    wide = jnp.dot(jnp.concatenate(columns, axis=0), hot, preferred_element_type=jnp.float32)
    blocks = [wide[b * states : (b + 1) * states] for b in range(len(columns))]
    return pick_block(tile_rows(row >> 8, states), blocks).astype(jnp.bfloat16)


def combine(total, back, surf, pot, newest, older, copies):
    last_step = copies > 0
    first_step = older is None
    states, nodes = newest.shape
    edge = surf.shape[1]
    vmem = pl.BlockSpec(memory_space=pltpu.VMEM)
    olds = () if first_step else (older,)
    if last_step:
        outs = [jax.ShapeDtypeStruct((2, copies, states, nodes // 2), jnp.bfloat16)]
    else:
        outs = [jax.ShapeDtypeStruct((states, n), jnp.bfloat16) for n in (nodes, edge)]
    return pl.pallas_call(
        functools.partial(combine_body, first_step, last_step),
        out_shape=outs,
        in_specs=[vmem] * (5 + len(olds)),
        out_specs=[vmem] * len(outs),
        cost_estimate=pl.CostEstimate(flops=1 << 28, bytes_accessed=1 << 20, transcendentals=0),
        compiler_params=pltpu.CompilerParams(vmem_limit_bytes=VMEM_LIMIT),
        name="combine",
    )(total, back, surf, pot, newest, *olds)


def edge_body(surf_ref, new_ref, out_ref):
    row = surf_ref[...]
    low16 = tile_rows(row & (LOW - 1), 16).astype(jnp.float32).astype(jnp.bfloat16)
    columns = [new_ref[:, b * LOW : (b + 1) * LOW] for b in range(new_ref.shape[1] // LOW)]
    out_ref[...] = edge_values(row, one_hot(low16), columns)


def edge(surf, newest):
    vmem = pl.BlockSpec(memory_space=pltpu.VMEM)
    return pl.pallas_call(
        edge_body,
        out_shape=jax.ShapeDtypeStruct((newest.shape[0], surf.shape[1]), jnp.bfloat16),
        in_specs=[vmem, vmem],
        out_specs=vmem,
        compiler_params=pltpu.CompilerParams(vmem_limit_bytes=VMEM_LIMIT),
        name="edge",
    )(surf, newest)


def split(a):
    upper = a.astype(jnp.bfloat16)
    return upper, (a - upper.astype(jnp.float32)).astype(jnp.bfloat16)


def product(a, b):
    rows = a.shape[0]
    (ah, al), (bh, bl) = split(a), split(b)
    dot = functools.partial(jnp.dot, preferred_element_type=jnp.float32)
    return dot(jnp.concatenate([ah, al, ah], axis=1), jnp.concatenate([bh, bh, bl], axis=0))


def own_rows(side_ref, ref, states):
    other = ref.shape[0] // 2
    start = pl.multiple_of(side_ref[1] * states, 16)
    return jnp.concatenate([ref[pl.ds(start, states), :], ref[pl.ds(start + other, states), :]], axis=0)


def gram_body(states, side_ref, field_ref, out_ref):
    rows = lax.dot_general(
        own_rows(side_ref, field_ref, states), field_ref[...], (((1,), (1,)), ((), ())),
        preferred_element_type=jnp.float32)
    depth = out_ref.shape[1]
    for i in range(out_ref.shape[0]):
        out_ref[i] = rows[i * depth : (i + 1) * depth]


def gram_rows(side, field, states, pieces):
    smem = pl.BlockSpec(memory_space=pltpu.SMEM)
    vmem = pl.BlockSpec(memory_space=pltpu.VMEM)
    return pl.pallas_call(
        functools.partial(gram_body, states),
        out_shape=jax.ShapeDtypeStruct((pieces, 2 * states // pieces, field.shape[0]), jnp.float32),
        in_specs=[smem, vmem],
        out_specs=vmem,
        compiler_params=pltpu.CompilerParams(vmem_limit_bytes=VMEM_LIMIT),
        name="gram",
    )(side, field)


def rotate_body(node_total, side_ref, here_ref, there_ref, field_ref, keep_ref, send_ref, high_ref, turned_ref):
    first = side_ref[2] == 0
    here, there = here_ref[...], there_ref[...]
    gram = jnp.concatenate([jnp.where(first, here, there), jnp.where(first, there, here)], axis=0)
    half = keep_ref.shape[0]
    scale_sum = jnp.sqrt(jnp.sum(gram * gram, keepdims=True)) + epsilon
    eye = (
        lax.broadcasted_iota(jnp.int32, gram.shape, 0) == lax.broadcasted_iota(jnp.int32, gram.shape, 1)
    ).astype(jnp.float32)
    growing = gram / scale_sum
    factor = 1.5 * eye - 0.5 * growing
    inverse = factor
    for iteration in range(1, ROOT_ITERS):
        growing = product(factor, growing)
        if iteration > 1:
            inverse = product(inverse, factor)
        factor = 1.5 * eye - 0.5 * product(growing, inverse)
    high_ref[...] = inverse
    mine = product(own_rows(side_ref, high_ref, half), factor)
    turn = (mine * jnp.sqrt(node_total / scale_sum)).astype(jnp.bfloat16)
    turned_ref[...] = jnp.dot(turn, field_ref[...], preferred_element_type=jnp.float32).astype(jnp.bfloat16)
    side = side_ref[0]
    keep_ref[...] = turned_ref[pl.ds(pl.multiple_of(side * half, 16), half), :]
    send_ref[...] = turned_ref[pl.ds(pl.multiple_of((1 - side) * half, 16), half), :]


def rotate(side, here, there, field, states, node_total):
    smem = pl.BlockSpec(memory_space=pltpu.SMEM)
    vmem = pl.BlockSpec(memory_space=pltpu.VMEM)
    total, nodes = field.shape
    return pl.pallas_call(
        functools.partial(rotate_body, node_total),
        out_shape=[jax.ShapeDtypeStruct((states, nodes), jnp.bfloat16)] * 2,
        in_specs=[smem, vmem, vmem, vmem],
        out_specs=[vmem] * 2,
        scratch_shapes=[pltpu.VMEM((total, total), jnp.float32), pltpu.VMEM((2 * states, nodes), jnp.bfloat16)],
        compiler_params=pltpu.CompilerParams(vmem_limit_bytes=VMEM_LIMIT),
        name="rotate",
    )(side, here, there, field)


def behind(block, distance):
    devices = range(lax.axis_size(DOM))
    route = [(i - distance, i) for i in devices if i - distance in devices]
    return lax.ppermute(block, DOM, route)


def swap(block, axes):
    return lax.all_to_all(block, axes, 0, 0, tiled=True)


def spread(block, axes):
    return swap(jnp.broadcast_to(block[None], (lax.axis_size(axes), *block.shape)), axes)


def gram_halves(rows):
    part = jnp.sum(swap(rows, ("core", "yl", "yh")), axis=0)
    part = jnp.sum(spread(part, "z"), axis=0)
    here = spread(part, ("x", "yl", "yh")).reshape(-1, rows.shape[-1])
    return here, turn_over(here, "core")


def turn_over(block, axis):
    return lax.ppermute(block, axis, [(0, 1), (1, 0)])


def body(orbitals, cell_matrix, connectivity, surface_nodes, cell_scale, potential):
    pot = potential[None, :]
    cell_args = (cell_scale, connectivity, cell_matrix)
    cell_count = connectivity.shape[0]
    inner = cell_count - cell_count // 4
    half = inner // 2
    side = jnp.stack([lax.axis_index(name) for name in ("yh", "x", "core")]).astype(jnp.int32)
    older, newest = None, orbitals
    boundary = edge(surface_nodes, newest)
    for degree_step in range(DEGREE):
        ghosts = behind(boundary, -1)
        first_total = cells(0, half, *cell_args, (newest,))
        shared = cells(inner, cell_count - inner, *cell_args, (newest, ghosts))
        returned = behind(shared[1], 1)
        total = cells(half, inner - half, *cell_args, (newest,), (first_total[0], shared[0]))[0]
        copies = lax.axis_size("x") if degree_step == DEGREE - 1 else 0
        result = combine(total, returned, surface_nodes, pot, newest, older, copies)
        older, newest = newest, result[0]
        boundary = result[-1]
    states, field = orbitals.shape[0], newest
    field = swap(field.reshape(-1, *field.shape[2:]), ST).reshape(-1, field.shape[3])
    pieces = lax.axis_size(("core", "yl", "yh"))
    here, there = gram_halves(gram_rows(side, field, states, pieces))
    node_total = lax.axis_size(DOM) * orbitals.shape[1]
    keep, send = rotate(side, here, there, field, states, node_total)
    other = turn_over(send, "yh")
    first = side[0] == 0
    return jnp.where(first, jnp.concatenate([keep, other], axis=1), jnp.concatenate([other, keep], axis=1))


DOM = ("z", "yl", "core")
ST = ("yh", "x")


def solution(mesh):
    dom, st = mesh.shape["dom"], mesh.shape["st"]
    fine = Mesh(mesh.devices.reshape(dom // 8, 4, 2, 2, st // 2), (*DOM, *ST))
    return jax.shard_map(
        body,
        mesh=fine,
        in_specs=(P(ST, DOM), P(), P(DOM, None), P(DOM, None), P(DOM), P(DOM)),
        out_specs=P(ST, DOM),
        check_vma=False,
    )
```

```python
import functools
import jax
import jax.numpy as jnp
from jax import lax
from jax.experimental import pallas as pl
from jax.experimental.pallas import tpu as pltpu
from jax.sharding import Mesh
from jax.sharding import PartitionSpec as P

DEGREE = 3
ROOT_ITERS = 4
LOW = 256
PARAMS = pltpu.CompilerParams(
    vmem_limit_bytes=24 << 20
)


center = 7.0
half_width = 6.0
epsilon = 1e-06


def tile_rows(row, rows):
    return jnp.broadcast_to(row, (rows, row.shape[1]))


def one_hot(low16):
    base = lax.broadcasted_iota(jnp.int32, low16.shape, 0)
    pieces = []
    for start in range(0, LOW, low16.shape[0]):
        ids = (base + start).astype(jnp.float32).astype(jnp.bfloat16)
        pieces.append(jnp.where(low16 == ids, jnp.bfloat16(1), jnp.bfloat16(0)))
    return jnp.concatenate(pieces, axis=0)


def pick_block(high, blocks):
    level, bit = list(blocks), 0
    while len(level) > 1:
        mask = (high >> bit) & 1 == 1
        nxt = []
        for i in range(0, len(level) - 1, 2):
            nxt.append(jnp.where(mask, level[i + 1], level[i]))
        if len(level) % 2:
            nxt.append(level[-1])
        level, bit = nxt, bit + 1
    return level[0]


def cells_body(n_add, first, count, n_blocks, scale_ref, *refs):
    conn_ref, matrix_ref = refs[0], refs[1]
    srcs = refs[2 : 2 + (2 if n_blocks > 8 else 1)]
    pos = 2 + len(srcs)
    adds = refs[pos : pos + n_add]
    out_refs = refs[pos + n_add : -2]
    oh_ref, got_ref = refs[-2:]
    states = srcs[0].shape[0]
    width = conn_ref.shape[1]
    columns = [srcs[0][:, b * LOW : (b + 1) * LOW] for b in range(srcs[0].shape[1] // LOW)]
    if n_blocks > 8:
        columns.append(srcs[1][...])
    stacked = jnp.concatenate(columns, axis=0)
    for i in range(count):
        row = conn_ref[first + i : first + i + 1, :]
        low16 = tile_rows(row & (LOW - 1), 16).astype(jnp.float32).astype(jnp.bfloat16)
        hot = one_hot(low16)
        oh_ref[i] = hot
        high = tile_rows(row >> 8, states)
        wide = jnp.dot(stacked, hot, preferred_element_type=jnp.float32)
        blocks = [wide[b * states : (b + 1) * states] for b in range(n_blocks)]
        got_ref[i * states : (i + 1) * states, :] = pick_block(high, blocks).astype(jnp.bfloat16)
    products = jnp.dot(got_ref[...], matrix_ref[...], preferred_element_type=jnp.float32)
    lefts = []
    for i in range(count):
        product = products[i * states : (i + 1) * states] * scale_ref[first + i]
        upper = product.astype(jnp.bfloat16)
        lower = (product - upper.astype(jnp.float32)).astype(jnp.bfloat16)
        row = conn_ref[first + i : first + i + 1, :]
        high16 = tile_rows(row >> 8, states).astype(jnp.float32).astype(jnp.bfloat16)
        zero = jnp.zeros_like(upper)
        masks = [high16 == jnp.bfloat16(b) for b in range(n_blocks)]
        lefts.append(jnp.concatenate([jnp.where(m, part, zero) for part in (upper, lower) for m in masks], axis=0))
    left = jnp.concatenate(lefts, axis=1)
    right = jnp.concatenate([oh_ref[i] for i in range(count)], axis=1)
    total = lax.dot_general(left, right, (((1,), (1,)), ((), ())), preferred_element_type=jnp.float32)
    total = total[: n_blocks * states] + total[n_blocks * states :]
    for b in range(n_blocks):
        value = total[b * states : (b + 1) * states]
        for a in adds:
            if b * LOW < a.shape[1]:
                value = value + a[:, b * LOW : (b + 1) * LOW]
        out_ref, place = (out_refs[0], b) if b < 8 else (out_refs[1], 0)
        out_ref[:, place * LOW : (place + 1) * LOW] = value


def cells(first, count, scale, conn, matrix, srcs, adds=()):
    states = srcs[0].shape[0]
    n_blocks = sum(s.shape[1] for s in srcs) // LOW
    smem = pl.BlockSpec(memory_space=pltpu.SMEM)
    vmem = pl.BlockSpec(memory_space=pltpu.VMEM)
    width = conn.shape[1]
    rows = states * n_blocks
    flops = 2 * count * width * (rows * LOW * 3 + states * width)
    return pl.pallas_call(
        functools.partial(cells_body, len(adds), first, count, n_blocks),
        out_shape=[jax.ShapeDtypeStruct(s.shape, jnp.float32) for s in srcs],
        in_specs=[smem] + [vmem] * (2 + len(srcs) + len(adds)),
        out_specs=[vmem] * len(srcs),
        scratch_shapes=[
            pltpu.VMEM((count, LOW, width), jnp.bfloat16),
            pltpu.VMEM((count * states, width), jnp.bfloat16),
        ],
        cost_estimate=pl.CostEstimate(flops=3 * flops, bytes_accessed=3 << 20, transcendentals=0),
        compiler_params=PARAMS,
        name=f"cells_{first}_{count}",
    )(scale, conn, matrix, *srcs, *adds)


def combine_body(first_step, last_step, total_ref, back_ref, surf_ref, pot_ref, new_ref, *refs):
    refs = list(refs)
    old_ref = None if first_step else refs.pop(0)
    out_ref = refs.pop(0)
    states, nodes = new_ref.shape
    n_blocks = nodes // LOW
    row = surf_ref[...]
    low16 = tile_rows(row & (LOW - 1), 16).astype(jnp.float32).astype(jnp.bfloat16)
    high16 = tile_rows(row >> 8, states).astype(jnp.float32).astype(jnp.bfloat16)
    hot = one_hot(low16)
    back = back_ref[...]
    upper = back.astype(jnp.bfloat16)
    lower = (back - upper.astype(jnp.float32)).astype(jnp.bfloat16)
    zero = jnp.zeros_like(upper)
    masks = [high16 == jnp.bfloat16(b) for b in range(n_blocks)]
    left = jnp.concatenate([jnp.where(m, part, zero) for part in (upper, lower) for m in masks], axis=0)
    added = lax.dot_general(left, hot, (((1,), (1,)), ((), ())), preferred_element_type=jnp.float32)
    added = added[: n_blocks * states] + added[n_blocks * states :]
    fresh_blocks = []
    for b in range(n_blocks):
        span = slice(b * LOW, (b + 1) * LOW)
        values = new_ref[:, span].astype(jnp.float32)
        image = total_ref[:, span] + added[b * states : (b + 1) * states]
        image = image + pot_ref[:, span] * values
        fresh = (image - center * values) / half_width
        if not first_step:
            fresh = 2.0 * fresh - old_ref[:, span].astype(jnp.float32)
        fresh = fresh.astype(jnp.bfloat16)
        if not last_step:
            out_ref[:, span] = fresh
        fresh_blocks.append(fresh)
    if last_step:
        middle = n_blocks // 2
        for part in range(2):
            block = jnp.concatenate(fresh_blocks[part * middle : (part + 1) * middle], axis=1)
            for copy in range(out_ref.shape[0]):
                out_ref[copy, part] = block
    else:
        refs[0][...] = edge_values(row, hot, fresh_blocks)


def edge_values(row, hot, columns):
    states = columns[0].shape[0]
    wide = jnp.dot(jnp.concatenate(columns, axis=0), hot, preferred_element_type=jnp.float32)
    blocks = [wide[b * states : (b + 1) * states] for b in range(len(columns))]
    return pick_block(tile_rows(row >> 8, states), blocks).astype(jnp.bfloat16)


def combine(total, back, surf, pot, newest, older, copies):
    last_step = copies > 0
    first_step = older is None
    states, nodes = newest.shape
    edge = surf.shape[1]
    vmem = pl.BlockSpec(memory_space=pltpu.VMEM)
    olds = () if first_step else (older,)
    if last_step:
        outs = [jax.ShapeDtypeStruct((copies, 2, states, nodes // 2), jnp.bfloat16)]
    else:
        outs = [jax.ShapeDtypeStruct((states, n), jnp.bfloat16) for n in (nodes, edge)]
    return pl.pallas_call(
        functools.partial(combine_body, first_step, last_step),
        out_shape=outs,
        in_specs=[vmem] * (5 + len(olds)),
        out_specs=[vmem] * len(outs),
        cost_estimate=pl.CostEstimate(flops=1 << 28, bytes_accessed=1 << 20, transcendentals=0),
        compiler_params=PARAMS,
        name="combine",
    )(total, back, surf, pot, newest, *olds)


def edge_body(surf_ref, new_ref, out_ref):
    row = surf_ref[...]
    low16 = tile_rows(row & (LOW - 1), 16).astype(jnp.float32).astype(jnp.bfloat16)
    columns = [new_ref[:, b * LOW : (b + 1) * LOW] for b in range(new_ref.shape[1] // LOW)]
    out_ref[...] = edge_values(row, one_hot(low16), columns)


def edge(surf, newest):
    vmem = pl.BlockSpec(memory_space=pltpu.VMEM)
    return pl.pallas_call(
        edge_body,
        out_shape=jax.ShapeDtypeStruct((newest.shape[0], surf.shape[1]), jnp.bfloat16),
        in_specs=[vmem, vmem],
        out_specs=vmem,
        compiler_params=PARAMS,
        name="edge",
    )(surf, newest)


def split(a):
    upper = a.astype(jnp.bfloat16)
    return upper, (a - upper.astype(jnp.float32)).astype(jnp.bfloat16)


def product(a, b):
    rows = a.shape[0]
    (ah, al), (bh, bl) = split(a), split(b)
    dot = functools.partial(jnp.dot, preferred_element_type=jnp.float32)
    return dot(jnp.concatenate([ah, al, ah], axis=1), jnp.concatenate([bh, bh, bl], axis=0))


def own_rows(side_ref, ref, rows):
    return ref[pl.ds(pl.multiple_of(side_ref[1] * rows, 32), rows), :]


def gram_body(rows, side_ref, field_ref, out_ref):
    mine = own_rows(side_ref, field_ref, rows)
    part = lax.dot_general(mine, field_ref[...], (((1,), (1,)), ((), ())), preferred_element_type=jnp.float32)
    for row, (i, span) in enumerate(pairs(out_ref, part.shape[1])):
        out_ref[i, :, span] = part[2 * row : 2 * row + 2]


def pairs(ref, columns):
    starts = range(0, ref.shape[2], columns)
    return [(i, slice(start, start + columns)) for i in range(ref.shape[0]) for start in starts]


def gram_rows(side, field, states, pieces):
    smem = pl.BlockSpec(memory_space=pltpu.SMEM)
    vmem = pl.BlockSpec(memory_space=pltpu.VMEM)
    return pl.pallas_call(
        functools.partial(gram_body, 2 * states),
        out_shape=jax.ShapeDtypeStruct((pieces, 2, states * field.shape[0] // pieces), jnp.float32),
        in_specs=[smem, vmem],
        out_specs=vmem,
        compiler_params=PARAMS,
        name="gram",
    )(side, field)


def rotate_body(node_total, side_ref, here_ref, there_ref, field_ref, keep_ref, send_ref, gram_ref, turned_ref):
    half, total = keep_ref.shape[0], gram_ref.shape[1]
    for core in range(2):

        @pl.when(side_ref[2] == core)
        def _():
            for ref, parity in ((here_ref, core), (there_ref, 1 - core)):
                for row, (i, span) in enumerate(pairs(ref, total)):
                    block, place = divmod(2 * row, half)
                    start = (2 * block + parity) * half + place
                    gram_ref[start : start + 2, :] = ref[i, :, span]

    gram = gram_ref[...]
    scale_sum = jnp.sqrt(jnp.sum(gram * gram, keepdims=True)) + epsilon
    eye = (
        lax.broadcasted_iota(jnp.int32, gram.shape, 0) == lax.broadcasted_iota(jnp.int32, gram.shape, 1)
    ).astype(jnp.float32)
    growing = gram / scale_sum
    factor = 1.5 * eye - 0.5 * growing
    inverse = factor
    for iteration in range(1, ROOT_ITERS):
        growing = product(factor, growing)
        if iteration > 1:
            inverse = product(inverse, factor)
        factor = 1.5 * eye - 0.5 * product(growing, inverse)
    gram_ref[...] = inverse
    mine = product(own_rows(side_ref, gram_ref, 2 * half), factor)
    turn = (mine * jnp.sqrt(node_total / scale_sum)).astype(jnp.bfloat16)
    turned_ref[...] = jnp.dot(turn, field_ref[...], preferred_element_type=jnp.float32).astype(jnp.bfloat16)
    side = side_ref[0]
    keep_ref[...] = turned_ref[pl.ds(pl.multiple_of(side * half, 16), half), :]
    send_ref[...] = turned_ref[pl.ds(pl.multiple_of((1 - side) * half, 16), half), :]


def rotate(side, here, there, field, states, node_total):
    smem = pl.BlockSpec(memory_space=pltpu.SMEM)
    vmem = pl.BlockSpec(memory_space=pltpu.VMEM)
    total, nodes = field.shape
    return pl.pallas_call(
        functools.partial(rotate_body, node_total),
        out_shape=[jax.ShapeDtypeStruct((states, nodes), jnp.bfloat16)] * 2,
        in_specs=[smem, vmem, vmem, vmem],
        out_specs=[vmem] * 2,
        scratch_shapes=[pltpu.VMEM((total, total), jnp.float32), pltpu.VMEM((2 * states, nodes), jnp.bfloat16)],
        compiler_params=PARAMS,
        name="rotate",
    )(side, here, there, field)


def behind(block, distance):
    devices = range(lax.axis_size(DOM))
    route = [(i - distance, i) for i in devices if i - distance in devices]
    return lax.ppermute(block, DOM, route)


def swap(block, axes):
    return lax.all_to_all(block, axes, 0, 0, tiled=True)


def spread(block, axes):
    return swap(jnp.broadcast_to(block[None], (lax.axis_size(axes), *block.shape)), axes)


def gram_halves(rows):
    part = jnp.sum(swap(rows, NEAR), axis=0)
    part = jnp.sum(spread(part, "z"), axis=0)
    here = spread(part, ("yh", "xh", "yl", "xl"))
    return here, turn_over(here, "core")


def turn_over(block, axis):
    return lax.ppermute(block, axis, [(0, 1), (1, 0)])


def body(orbitals, cell_matrix, connectivity, surface_nodes, cell_scale, potential):
    pot = potential[None, :]
    cell_args = (cell_scale, connectivity, cell_matrix)
    cell_count = connectivity.shape[0]
    inner = cell_count - cell_count // 4
    half = inner // 2
    side = jnp.stack([lax.axis_index(name) for name in ("xl", ("yh", "xh"), "core")]).astype(jnp.int32)
    older, newest = None, orbitals
    boundary = edge(surface_nodes, newest)
    for degree_step in range(DEGREE):
        ghosts = behind(boundary, -1)
        first_total = cells(0, half, *cell_args, (newest,))
        shared = cells(inner, cell_count - inner, *cell_args, (newest, ghosts))
        returned = behind(shared[1], 1)
        total = cells(half, inner - half, *cell_args, (newest,), (first_total[0], shared[0]))[0]
        copies = lax.axis_size(("yh", "xh")) if degree_step == DEGREE - 1 else 0
        result = combine(total, returned, surface_nodes, pot, newest, older, copies)
        older, newest = newest, result[0]
        boundary = result[-1]
    states, field = orbitals.shape[0], newest
    field = swap(field.reshape(-1, *field.shape[2:]), ST).reshape(-1, field.shape[3])
    pieces = lax.axis_size(NEAR)
    here, there = gram_halves(gram_rows(side, field, states, pieces))
    node_total = lax.axis_size(DOM) * orbitals.shape[1]
    keep, send = rotate(side, here, there, field, states, node_total)
    other = turn_over(send, "xl")
    first = side[0] == 0
    return jnp.where(first, jnp.concatenate([keep, other], axis=1), jnp.concatenate([other, keep], axis=1))


DOM = ("z", "yl", "core")
ST = ("yh", "xh", "xl")
NEAR = ("core", "yl", "xl")


def solution(mesh):
    dom, st = mesh.shape["dom"], mesh.shape["st"]
    fine = Mesh(mesh.devices.reshape(dom // 8, 4, 2, 2, st // 4, 2), (*DOM, *ST))
    return jax.shard_map(
        body,
        mesh=fine,
        in_specs=(P(ST, DOM), P(), P(DOM, None), P(DOM, None), P(DOM), P(DOM)),
        out_specs=P(ST, DOM),
        check_vma=False,
    )
```

```python
import functools
import jax
import jax.numpy as jnp
from jax import lax
from jax.experimental import pallas as pl
from jax.experimental.pallas import tpu as pltpu
from jax.sharding import Mesh
from jax.sharding import PartitionSpec as P

DEGREE = 3
ROOT_ITERS = 4
LOW = 256
PARAMS = pltpu.CompilerParams(
    vmem_limit_bytes=24 << 20
)


center = 7.0
half_width = 6.0
epsilon = 1e-06


def tile_rows(row, rows):
    return jnp.broadcast_to(row, (rows, row.shape[1]))


def one_hot(low16):
    base = lax.broadcasted_iota(jnp.int32, low16.shape, 0)
    pieces = []
    for start in range(0, LOW, low16.shape[0]):
        ids = (base + start).astype(jnp.float32).astype(jnp.bfloat16)
        pieces.append(jnp.where(low16 == ids, jnp.bfloat16(1), jnp.bfloat16(0)))
    return jnp.concatenate(pieces, axis=0)


def pick_block(high, blocks):
    level, bit = list(blocks), 0
    while len(level) > 1:
        mask = (high >> bit) & 1 == 1
        nxt = []
        for i in range(0, len(level) - 1, 2):
            nxt.append(jnp.where(mask, level[i + 1], level[i]))
        if len(level) % 2:
            nxt.append(level[-1])
        level, bit = nxt, bit + 1
    return level[0]


def cells_body(n_add, first, count, n_blocks, scale_ref, *refs):
    conn_ref, matrix_ref = refs[0], refs[1]
    srcs = refs[2 : 2 + (2 if n_blocks > 8 else 1)]
    pos = 2 + len(srcs)
    adds = refs[pos : pos + n_add]
    out_refs = refs[pos + n_add : -2]
    oh_ref, got_ref = refs[-2:]
    states = srcs[0].shape[0]
    width = conn_ref.shape[1]
    columns = [srcs[0][:, b * LOW : (b + 1) * LOW] for b in range(srcs[0].shape[1] // LOW)]
    if n_blocks > 8:
        columns.append(srcs[1][...])
    stacked = jnp.concatenate(columns, axis=0)
    for i in range(count):
        row = conn_ref[first + i : first + i + 1, :]
        low16 = tile_rows(row & (LOW - 1), 16).astype(jnp.float32).astype(jnp.bfloat16)
        hot = one_hot(low16)
        oh_ref[i] = hot
        high = tile_rows(row >> 8, states)
        wide = jnp.dot(stacked, hot, preferred_element_type=jnp.float32)
        blocks = [wide[b * states : (b + 1) * states] for b in range(n_blocks)]
        got_ref[i * states : (i + 1) * states, :] = pick_block(high, blocks).astype(jnp.bfloat16)
    products = jnp.dot(got_ref[...], matrix_ref[...], preferred_element_type=jnp.float32)
    lefts = []
    for i in range(count):
        product = products[i * states : (i + 1) * states] * scale_ref[first + i]
        upper = product.astype(jnp.bfloat16)
        lower = (product - upper.astype(jnp.float32)).astype(jnp.bfloat16)
        row = conn_ref[first + i : first + i + 1, :]
        high16 = tile_rows(row >> 8, states).astype(jnp.float32).astype(jnp.bfloat16)
        zero = jnp.zeros_like(upper)
        masks = [high16 == jnp.bfloat16(b) for b in range(n_blocks)]
        lefts.append(jnp.concatenate([jnp.where(m, part, zero) for part in (upper, lower) for m in masks], axis=0))
    left = jnp.concatenate(lefts, axis=1)
    right = jnp.concatenate([oh_ref[i] for i in range(count)], axis=1)
    total = lax.dot_general(left, right, (((1,), (1,)), ((), ())), preferred_element_type=jnp.float32)
    total = total[: n_blocks * states] + total[n_blocks * states :]
    for b in range(n_blocks):
        value = total[b * states : (b + 1) * states]
        for a in adds:
            if b * LOW < a.shape[1]:
                value = value + a[:, b * LOW : (b + 1) * LOW]
        out_ref, place = (out_refs[0], b) if b < 8 else (out_refs[1], 0)
        out_ref[:, place * LOW : (place + 1) * LOW] = value


def cells(first, count, scale, conn, matrix, srcs, adds=()):
    states = srcs[0].shape[0]
    n_blocks = sum(s.shape[1] for s in srcs) // LOW
    smem = pl.BlockSpec(memory_space=pltpu.SMEM)
    vmem = pl.BlockSpec(memory_space=pltpu.VMEM)
    width = conn.shape[1]
    rows = states * n_blocks
    flops = 2 * count * width * (rows * LOW * 3 + states * width)
    return pl.pallas_call(
        functools.partial(cells_body, len(adds), first, count, n_blocks),
        out_shape=[jax.ShapeDtypeStruct(s.shape, jnp.float32) for s in srcs],
        in_specs=[smem] + [vmem] * (2 + len(srcs) + len(adds)),
        out_specs=[vmem] * len(srcs),
        scratch_shapes=[
            pltpu.VMEM((count, LOW, width), jnp.bfloat16),
            pltpu.VMEM((count * states, width), jnp.bfloat16),
        ],
        cost_estimate=pl.CostEstimate(flops=3 * flops, bytes_accessed=3 << 20, transcendentals=0),
        compiler_params=PARAMS,
        name=f"cells_{first}_{count}",
    )(scale, conn, matrix, *srcs, *adds)


def combine_body(first_step, last_step, total_ref, back_ref, surf_ref, pot_ref, new_ref, *refs):
    refs = list(refs)
    old_ref = None if first_step else refs.pop(0)
    out_ref = refs.pop(0)
    states, nodes = new_ref.shape
    n_blocks = nodes // LOW
    row = surf_ref[...]
    low16 = tile_rows(row & (LOW - 1), 16).astype(jnp.float32).astype(jnp.bfloat16)
    high16 = tile_rows(row >> 8, states).astype(jnp.float32).astype(jnp.bfloat16)
    hot = one_hot(low16)
    back = back_ref[...]
    upper = back.astype(jnp.bfloat16)
    lower = (back - upper.astype(jnp.float32)).astype(jnp.bfloat16)
    zero = jnp.zeros_like(upper)
    masks = [high16 == jnp.bfloat16(b) for b in range(n_blocks)]
    left = jnp.concatenate([jnp.where(m, part, zero) for part in (upper, lower) for m in masks], axis=0)
    added = lax.dot_general(left, hot, (((1,), (1,)), ((), ())), preferred_element_type=jnp.float32)
    added = added[: n_blocks * states] + added[n_blocks * states :]
    fresh_blocks = []
    for b in range(n_blocks):
        span = slice(b * LOW, (b + 1) * LOW)
        values = new_ref[:, span].astype(jnp.float32)
        image = total_ref[:, span] + added[b * states : (b + 1) * states]
        image = image + pot_ref[:, span] * values
        fresh = (image - center * values) / half_width
        if not first_step:
            fresh = 2.0 * fresh - old_ref[:, span].astype(jnp.float32)
        fresh = fresh.astype(jnp.bfloat16)
        if not last_step:
            out_ref[:, span] = fresh
        fresh_blocks.append(fresh)
    if last_step:
        middle = n_blocks // 2
        for part in range(2):
            block = jnp.concatenate(fresh_blocks[part * middle : (part + 1) * middle], axis=1)
            for copy in range(out_ref.shape[0]):
                out_ref[copy, part] = block
    else:
        refs[0][...] = edge_values(row, hot, fresh_blocks)


def edge_values(row, hot, columns):
    states = columns[0].shape[0]
    wide = jnp.dot(jnp.concatenate(columns, axis=0), hot, preferred_element_type=jnp.float32)
    blocks = [wide[b * states : (b + 1) * states] for b in range(len(columns))]
    return pick_block(tile_rows(row >> 8, states), blocks).astype(jnp.bfloat16)


def combine(total, back, surf, pot, newest, older, copies):
    last_step = copies > 0
    first_step = older is None
    states, nodes = newest.shape
    edge = surf.shape[1]
    vmem = pl.BlockSpec(memory_space=pltpu.VMEM)
    olds = () if first_step else (older,)
    if last_step:
        outs = [jax.ShapeDtypeStruct((copies, 2, states, nodes // 2), jnp.bfloat16)]
    else:
        outs = [jax.ShapeDtypeStruct((states, n), jnp.bfloat16) for n in (nodes, edge)]
    return pl.pallas_call(
        functools.partial(combine_body, first_step, last_step),
        out_shape=outs,
        in_specs=[vmem] * (5 + len(olds)),
        out_specs=[vmem] * len(outs),
        cost_estimate=pl.CostEstimate(flops=1 << 28, bytes_accessed=1 << 20, transcendentals=0),
        compiler_params=PARAMS,
        name="combine",
    )(total, back, surf, pot, newest, *olds)


def edge_body(surf_ref, new_ref, out_ref):
    row = surf_ref[...]
    low16 = tile_rows(row & (LOW - 1), 16).astype(jnp.float32).astype(jnp.bfloat16)
    columns = [new_ref[:, b * LOW : (b + 1) * LOW] for b in range(new_ref.shape[1] // LOW)]
    out_ref[...] = edge_values(row, one_hot(low16), columns)


def edge(surf, newest):
    vmem = pl.BlockSpec(memory_space=pltpu.VMEM)
    return pl.pallas_call(
        edge_body,
        out_shape=jax.ShapeDtypeStruct((newest.shape[0], surf.shape[1]), jnp.bfloat16),
        in_specs=[vmem, vmem],
        out_specs=vmem,
        compiler_params=PARAMS,
        name="edge",
    )(surf, newest)


def split(a):
    upper = a.astype(jnp.bfloat16)
    return upper, (a - upper.astype(jnp.float32)).astype(jnp.bfloat16)


def widths(a, b):
    (ah, al), (bh, bl) = split(a), split(b)
    return jnp.concatenate([ah, al, ah], axis=1), jnp.concatenate([bh, bh, bl], axis=0)


def product(a, b):
    left, right = widths(a, b)
    return jnp.dot(left, right, preferred_element_type=jnp.float32)


def symmetric_product(a, b):
    left, right = widths(a, b)
    main = jnp.dot(left, right[:, :LOW], preferred_element_type=jnp.float32)
    corner = jnp.dot(left[LOW:], right[:, LOW:], preferred_element_type=jnp.float32)
    return jnp.concatenate([main, jnp.concatenate([main[LOW:].T, corner], axis=0)], axis=1)


def own_rows(side_ref, ref, rows):
    return ref[pl.ds(pl.multiple_of(side_ref[1] * rows, 32), rows), :]


def gram_body(rows, side_ref, field_ref, out_ref):
    mine = own_rows(side_ref, field_ref, rows)
    part = lax.dot_general(mine, field_ref[...], (((1,), (1,)), ((), ())), preferred_element_type=jnp.float32)
    for row, (i, span) in enumerate(pairs(out_ref, part.shape[1])):
        out_ref[i, :, span] = part[2 * row : 2 * row + 2]


def pairs(ref, columns):
    starts = range(0, ref.shape[2], columns)
    return [(i, slice(start, start + columns)) for i in range(ref.shape[0]) for start in starts]


def gram_rows(side, field, states, pieces):
    smem = pl.BlockSpec(memory_space=pltpu.SMEM)
    vmem = pl.BlockSpec(memory_space=pltpu.VMEM)
    return pl.pallas_call(
        functools.partial(gram_body, 2 * states),
        out_shape=jax.ShapeDtypeStruct((pieces, 2, states * field.shape[0] // pieces), jnp.float32),
        in_specs=[smem, vmem],
        out_specs=vmem,
        compiler_params=PARAMS,
        name="gram",
    )(side, field)


def rotate_body(node_total, side_ref, here_ref, there_ref, field_ref, keep_ref, send_ref, gram_ref, turned_ref):
    half, total = keep_ref.shape[0], gram_ref.shape[1]
    for core in range(2):

        @pl.when(side_ref[2] == core)
        def _():
            for ref, parity in ((here_ref, core), (there_ref, 1 - core)):
                for row, (i, span) in enumerate(pairs(ref, total)):
                    block, place = divmod(2 * row, half)
                    start = (2 * block + parity) * half + place
                    gram_ref[start : start + 2, :] = ref[i, :, span]

    gram = gram_ref[...]
    scale_sum = jnp.sqrt(jnp.sum(gram * gram, keepdims=True)) + epsilon
    eye = (
        lax.broadcasted_iota(jnp.int32, gram.shape, 0) == lax.broadcasted_iota(jnp.int32, gram.shape, 1)
    ).astype(jnp.float32)
    growing = gram / scale_sum
    factor = 1.5 * eye - 0.5 * growing
    inverse = factor
    for iteration in range(1, ROOT_ITERS):
        growing = symmetric_product(factor, growing)
        if iteration > 1:
            inverse = symmetric_product(inverse, factor)
        factor = 1.5 * eye - 0.5 * symmetric_product(growing, inverse)
    gram_ref[...] = inverse
    mine = product(own_rows(side_ref, gram_ref, 2 * half), factor)
    turn = (mine * jnp.sqrt(node_total / scale_sum)).astype(jnp.bfloat16)
    turned_ref[...] = jnp.dot(turn, field_ref[...], preferred_element_type=jnp.float32).astype(jnp.bfloat16)
    side = side_ref[0]
    keep_ref[...] = turned_ref[pl.ds(pl.multiple_of(side * half, 16), half), :]
    send_ref[...] = turned_ref[pl.ds(pl.multiple_of((1 - side) * half, 16), half), :]


def rotate(side, here, there, field, states, node_total):
    smem = pl.BlockSpec(memory_space=pltpu.SMEM)
    vmem = pl.BlockSpec(memory_space=pltpu.VMEM)
    total, nodes = field.shape
    return pl.pallas_call(
        functools.partial(rotate_body, node_total),
        out_shape=[jax.ShapeDtypeStruct((states, nodes), jnp.bfloat16)] * 2,
        in_specs=[smem, vmem, vmem, vmem],
        out_specs=[vmem] * 2,
        scratch_shapes=[pltpu.VMEM((total, total), jnp.float32), pltpu.VMEM((2 * states, nodes), jnp.bfloat16)],
        compiler_params=PARAMS,
        name="rotate",
    )(side, here, there, field)


def behind(block, distance):
    devices = range(lax.axis_size(DOM))
    route = [(i - distance, i) for i in devices if i - distance in devices]
    return lax.ppermute(block, DOM, route)


def swap(block, axes):
    return lax.all_to_all(block, axes, 0, 0, tiled=True)


def spread(block, axes):
    return swap(jnp.broadcast_to(block[None], (lax.axis_size(axes), *block.shape)), axes)


def gram_halves(rows):
    part = jnp.sum(swap(rows, NEAR), axis=0)
    part = jnp.sum(spread(part, "z"), axis=0)
    here = spread(part, ("yh", "xh", "yl", "xl"))
    return here, turn_over(here, "core")


def turn_over(block, axis):
    return lax.ppermute(block, axis, [(0, 1), (1, 0)])


def body(orbitals, cell_matrix, connectivity, surface_nodes, cell_scale, potential):
    pot = potential[None, :]
    cell_args = (cell_scale, connectivity, cell_matrix)
    cell_count = connectivity.shape[0]
    inner = cell_count - cell_count // 4
    half = inner // 2
    side = jnp.stack([lax.axis_index(name) for name in ("xl", ("yh", "xh"), "core")]).astype(jnp.int32)
    older, newest = None, orbitals
    boundary = edge(surface_nodes, newest)
    for degree_step in range(DEGREE):
        ghosts = behind(boundary, -1)
        first_total = cells(0, half, *cell_args, (newest,))
        shared = cells(inner, cell_count - inner, *cell_args, (newest, ghosts))
        returned = behind(shared[1], 1)
        total = cells(half, inner - half, *cell_args, (newest,), (first_total[0], shared[0]))[0]
        copies = lax.axis_size(("yh", "xh")) if degree_step == DEGREE - 1 else 0
        result = combine(total, returned, surface_nodes, pot, newest, older, copies)
        older, newest = newest, result[0]
        boundary = result[-1]
    states, field = orbitals.shape[0], newest
    field = swap(field.reshape(-1, *field.shape[2:]), ST).reshape(-1, field.shape[3])
    pieces = lax.axis_size(NEAR)
    here, there = gram_halves(gram_rows(side, field, states, pieces))
    node_total = lax.axis_size(DOM) * orbitals.shape[1]
    keep, send = rotate(side, here, there, field, states, node_total)
    other = turn_over(send, "xl")
    first = side[0] == 0
    return jnp.where(first, jnp.concatenate([keep, other], axis=1), jnp.concatenate([other, keep], axis=1))


DOM = ("z", "yl", "core")
ST = ("yh", "xh", "xl")
NEAR = ("core", "yl", "xl")


def solution(mesh):
    dom, st = mesh.shape["dom"], mesh.shape["st"]
    fine = Mesh(mesh.devices.reshape(dom // 8, 4, 2, 2, st // 4, 2), (*DOM, *ST))
    return jax.shard_map(
        body,
        mesh=fine,
        in_specs=(P(ST, DOM), P(), P(DOM, None), P(DOM, None), P(DOM), P(DOM)),
        out_specs=P(ST, DOM),
        check_vma=False,
    )
```
